32 devices in a mesh: sa: 8 (over z, y), col: 2 (over x), af: 2 (over core).
Axes of the slice: x: 2, y: 2, z: 4, core: 2. Of those that a mesh axis runs over, the one named last changes fastest.
Arguments:
- scan_volume: bfloat16 [256, 32, 8, 128], P('col', 'sa'), may hold values from -6 to 6
- conv_kernel: bfloat16 [27, 256, 256], P(None, 'col', 'af'), may hold values from -0.078125 to 0.078125
- out_cotangent: bfloat16 [256, 32, 8, 128], P('af', 'sa', 'col'), may hold values from -6 to 6
Outputs:
- activation: bfloat16 [256, 32, 8, 128], P('af', 'sa', 'col')
- volume_grad: bfloat16 [256, 32, 8, 128], P('col', 'sa', 'af')
- kernel_grad: float32 [27, 256, 256], P(None, 'col', 'af')
The draws below stay inside these ranges and needn't reach their ends.
All inputs are finite; a program needn't handle non-finite values.
Results may differ from the reference program's by a relative error of at most 0.001.
Values may be sent and summed in bfloat16 or wider, within the bound.
A program may use at most 128 MiB of HBM per device.

```python
import jax
import jax.numpy as jnp

C = 256
F = 256
ROWS = 8
COLS = 128
DEPTH = 32


def block_scale(key, dims, split, low, high):
    gain, own = 1.0, jax.random.fold_in(key, 6)
    for position, parts in split:
        heights = jnp.exp(jax.random.uniform(jax.random.fold_in(own, position), (parts,), jnp.float32, low / len(split), high / len(split)))
        gain = gain * jnp.repeat(heights, dims[position] // parts).reshape([-1 if axis == position else 1 for axis in range(len(dims))])
    return gain


def bell_draw(stream_key, dims, scale, most, cuts=(), kind=jnp.bfloat16):
    array = scale * jax.random.normal(stream_key, dims, jnp.float32)
    if cuts:
        array = array * block_scale(stream_key, dims, cuts, -0.22, 0.18)
    return jnp.clip(array, -most, most).astype(kind)


def setup_inputs(seed: int = 0) -> dict:
    streams_of = jax.random.split(jax.random.key(seed), 4)
    return {
        "scan_volume": bell_draw(streams_of[0], (C, DEPTH, ROWS, COLS), 1.0, 6.0, ((0, 2), (1, 8))),
        "conv_kernel": bell_draw(streams_of[1], (27, C, F), (27 * C) ** -0.5, 0.078125, ((1, 2), (2, 2))),
        "out_cotangent": bell_draw(streams_of[2], (F, DEPTH, ROWS, COLS), 1.0, 6.0, ((0, 2), (1, 8), (2, 2))),
    }


def reference(scan_volume, conv_kernel, out_cotangent):
    pads = ((0, 0), (1, 1), (1, 1), (1, 1))
    vol_pad = jnp.pad(scan_volume, pads)
    grad_pad = jnp.pad(out_cotangent, pads)
    kernel_wide = conv_kernel.astype(jnp.float32)
    grad_wide = out_cotangent.astype(jnp.float32)
    activation = jnp.zeros((F, DEPTH, ROWS, COLS), jnp.float32)
    volume_grad = jnp.zeros((C, DEPTH, ROWS, COLS), jnp.float32)
    grads_list = []
    for tap_index in range(27):
        depth_step = tap_index // 9
        row_step = (tap_index // 3) % 3
        col_step = tap_index % 3
        window = vol_pad[:, depth_step:depth_step + DEPTH, row_step:row_step + ROWS, col_step:col_step + COLS].astype(jnp.float32)
        activation = activation + jnp.einsum("cf,cdhw->fdhw", kernel_wide[tap_index], window)
        behind = grad_pad[:, 2 - depth_step:2 - depth_step + DEPTH, 2 - row_step:2 - row_step + ROWS, 2 - col_step:2 - col_step + COLS].astype(jnp.float32)
        volume_grad = volume_grad + jnp.einsum("cf,fdhw->cdhw", kernel_wide[tap_index], behind)
        grads_list.append(jnp.einsum("cdhw,fdhw->cf", window, grad_wide))
    kernel_grad = jnp.stack(grads_list) * (float(DEPTH * ROWS * COLS) ** -0.5)
    return activation.astype(jnp.bfloat16), volume_grad.astype(jnp.bfloat16), kernel_grad
```

```python
import functools

import jax
import jax.numpy as jnp
from jax import lax
from jax.experimental import pallas as pl
from jax.experimental.pallas import tpu as pltpu
from jax.sharding import PartitionSpec as P


def extended(value, sides, width):
    for axis, dim in sides:
        size, length = (lax.axis_size(axis), value.shape[dim])
        up = [(i, (i + 1) % size) for i in range(size - 1)]
        down = [(j, i) for i, j in up]
        last = lax.slice_in_dim(value, length - width, length, axis=dim)
        first = lax.slice_in_dim(value, 0, width, axis=dim)
        before = lax.ppermute(last, axis, up)
        after = lax.ppermute(first, axis, down)
        value = jnp.concatenate([before, value, after], axis=dim)
    return value


def forward_taps(padded, kernel_block, slab_depth, slab_rows, slab_width):
    channels = padded.shape[0]
    filters = kernel_block.shape[2]
    accumulated = jnp.zeros((filters, slab_depth, slab_rows, slab_width), jnp.float32)
    for depth_step in range(3):
        shifted = jnp.concatenate(
            [
                padded[
                    :,
                    depth_step : depth_step + slab_depth,
                    row_step : row_step + slab_rows,
                    col_step : col_step + slab_width,
                ]
                for row_step in range(3)
                for col_step in range(3)
            ],
            axis=0,
        )
        matrix = kernel_block[9 * depth_step : 9 * depth_step + 9].reshape(9 * channels, filters)
        accumulated = accumulated + jnp.einsum(
            "kf,kdhw->fdhw", matrix, shifted, preferred_element_type=jnp.float32
        )
    return accumulated


def backward_taps(grad_pad, kernel_block, slab_depth, slab_rows, slab_width):
    channels = kernel_block.shape[1]
    filters = kernel_block.shape[2]
    accumulated = jnp.zeros((channels, slab_depth, slab_rows, slab_width), jnp.float32)
    for depth_step in range(3):
        shifted = jnp.concatenate(
            [
                grad_pad[
                    :,
                    2 - depth_step : 2 - depth_step + slab_depth,
                    2 - row_step : 2 - row_step + slab_rows,
                    2 - col_step : 2 - col_step + slab_width,
                ]
                for row_step in range(3)
                for col_step in range(3)
            ],
            axis=0,
        )
        matrix = jnp.swapaxes(kernel_block[9 * depth_step : 9 * depth_step + 9], 1, 2).reshape(
            9 * filters, channels
        )
        accumulated = accumulated + jnp.einsum(
            "kc,kdhw->cdhw", matrix, shifted, preferred_element_type=jnp.float32
        )
    return accumulated


def weight_taps(padded, grad_slab, slab_depth, slab_rows, slab_width):
    channels = padded.shape[0]
    filters = grad_slab.shape[0]
    pieces = []
    for depth_step in range(3):
        shifted = jnp.concatenate(
            [
                padded[
                    :,
                    depth_step : depth_step + slab_depth,
                    row_step : row_step + slab_rows,
                    col_step : col_step + slab_width,
                ]
                for row_step in range(3)
                for col_step in range(3)
            ],
            axis=0,
        )
        product = jnp.einsum(
            "kdhw,fdhw->kf", shifted, grad_slab, preferred_element_type=jnp.float32
        )
        pieces.append(product.reshape(9, channels, filters))
    return jnp.concatenate(pieces, axis=0)


def per_device(scan_volume, conv_kernel, out_cotangent):
    slab_depth = scan_volume.shape[1]
    slab_rows = scan_volume.shape[2]
    slab_width = scan_volume.shape[3]
    with_rim = extended(scan_volume, (("sa", 1),), 1)
    padded_vol = jnp.pad(with_rim, ((0, 0), (0, 0), (1, 1), (1, 1)))
    partial_out = forward_taps(padded_vol, conv_kernel, slab_depth, slab_rows, slab_width)
    summed = lax.psum_scatter(partial_out, "col", scatter_dimension=2, tiled=True)
    activation = summed.astype(jnp.bfloat16)
    grad_slab = lax.all_gather(out_cotangent, "col", axis=2, tiled=True)
    grad_rim = extended(grad_slab, (("sa", 1),), 1)
    grad_pad = jnp.pad(grad_rim, ((0, 0), (0, 0), (1, 1), (1, 1)))
    volume_partial = backward_taps(grad_pad, conv_kernel, slab_depth, slab_rows, slab_width)
    volume_grad = lax.psum_scatter(volume_partial, "af", scatter_dimension=2, tiled=True).astype(
        jnp.bfloat16
    )
    weight_partial = weight_taps(padded_vol, grad_slab, slab_depth, slab_rows, slab_width)
    factor = float(slab_depth * lax.axis_size("sa") * slab_rows * slab_width) ** (-0.5)
    kernel_grad = lax.psum(weight_partial, "sa") * factor
    return (activation, volume_grad, kernel_grad)


MESH = pl.DeviceIdType.MESH
TAP_ROWS = 1152
PIECE_START = (0, 640, 1152, 1792, 2304, 2944)
PIECE_ROWS = (640, 512, 640, 512, 640, 512)
KG_POWER, ACT_POWER = 9, 17
TOP = 124.0


def code_scale(peak):
    return jnp.maximum(peak, 2.0 ** -90).astype(jnp.bfloat16)


def encode(value, scale, power):
    x = value * ((2.0 ** (TOP / power)) / scale)
    x2 = x * x
    x4 = x2 * x2
    x8 = x4 * x4
    high = x8 if power == 9 else x8 * x8
    return (high * x).astype(jnp.bfloat16)


def decode(code, scale, power):
    wide = code.astype(jnp.float32)
    size = jnp.exp2(jnp.log(jnp.abs(wide)) * (1.0 / (power * 0.6931471805599453)))
    size = jnp.where(wide == 0.0, 0.0, size) * (scale * (2.0 ** (-TOP / power)))
    return jnp.where(wide < 0.0, -size, size)


def tiles(value):
    return value.reshape(value.shape[0] // 8, 8, 128)


def fused_kernel(factor, vol_ref, cot_ref, w_ref, act_ref, vgrad_ref, kg_ref,
                 cot_in, rim_own, rim_other, wf_ref, wb_ref, xs, gs, gb, part, kgb, e_y, e_n, e_f, r_y, r_n, r_f, s_kg,
                 a_out, a_send, a_in, b_out, b_in,
                 s_sem, r_sem, fs_sem, fr_sem, bs_sem, br_sem, cs_sem, cr_sem, hs_sem, hr_sem):
    sa = lax.axis_index("sa")
    col = lax.axis_index("col")
    af = lax.axis_index("af")
    y, z0, z1 = sa % 2, (sa // 2) % 2, sa // 4
    to_y = (sa + 1 - 2 * y, col, af)
    to_n = (sa + 2 - 4 * z0, col, af)
    to_f = (sa + 4 - 8 * z1, col, af)
    to_col = (sa, 1 - col, af)
    to_af = (sa, col, 1 - af)

    low, high = sa > 0, sa < 7
    diagonal = sa - 1 + 2 * y
    has_diagonal = jnp.logical_and(diagonal >= 0, diagonal <= 7)

    barrier = pltpu.get_barrier_semaphore()
    for device in (to_y, to_n, to_f, to_col, to_af):
        pl.semaphore_signal(barrier, inc=1, device_id=device, device_id_type=MESH)

    @pl.when(has_diagonal)
    def _():
        pl.semaphore_signal(barrier, inc=1, device_id=(diagonal, col, af), device_id_type=MESH)

    pl.semaphore_wait(barrier, 5 + has_diagonal.astype(jnp.int32))

    cot_copy = pltpu.make_async_remote_copy(
        src_ref=cot_ref, dst_ref=cot_in, send_sem=cs_sem, recv_sem=cr_sem,
        device_id=to_col, device_id_type=MESH)
    cot_copy.start()

    def plane_at(p):
        return pl.ds(pl.multiple_of(p * 1024, 1024), 1024)

    def send(which, source, target, device):
        return pltpu.make_async_remote_copy(
            src_ref=source, dst_ref=target, send_sem=hs_sem.at[which], recv_sem=hr_sem.at[which],
            device_id=device, device_id_type=MESH)

    above, below = (sa + 1, col, af), (sa - 1, col, af)
    half = pl.ds(pl.multiple_of(128 + af * 64, 64), 64)
    vol_up = send(0, xs.at[half, 4096:5120], xs.at[half, 0:1024], above)
    vol_down = send(1, xs.at[half, 1024:2048], xs.at[half, 5120:6144], below)
    vol_pass = (send(2, xs.at[half, 0:1024], xs.at[half, 0:1024], to_af),
                send(3, xs.at[half, 5120:6144], xs.at[half, 5120:6144], to_af))
    cot_up = send(4, cot_ref.at[:, 3], rim_own.at[0], above)
    cot_down = send(5, cot_ref.at[:, 0], rim_own.at[1], below)
    cot_pass = (send(6, rim_own.at[0], rim_other.at[0], to_col),
                send(7, rim_own.at[1], rim_other.at[1], to_col))

    def start_rims(up, down):
        pl.when(high)(up.start)
        pl.when(low)(down.start)

    def relay_rims(up, down, onward):
        @pl.when(low)
        def _():
            up.wait_recv()
            onward[0].start()

        @pl.when(high)
        def _():
            down.wait_recv()
            onward[1].start()

    def finish_rims(up, down, onward):
        pl.when(high)(up.wait_send)
        pl.when(low)(down.wait_send)
        pl.when(low)(onward[0].wait)
        pl.when(high)(onward[1].wait)

    def clear_edges(stacked):
        @pl.when(sa == 0)
        def _():
            stacked[128:256, 0:1024] = jnp.zeros((128, 1024), jnp.bfloat16)

        @pl.when(sa == 7)
        def _():
            stacked[128:256, 5120:6144] = jnp.zeros((128, 1024), jnp.bfloat16)

    lane = lax.broadcasted_iota(jnp.int32, (128, 1024), 1) % 128

    def spread(target, first, count, step, before_row, after_row):
        def plane(i, carry):
            at = plane_at(first + i * step)
            wide = target[128:256, at].astype(jnp.float32)
            before = jnp.where(lane == 0, 0.0, pltpu.roll(wide, 1, 1))
            after = jnp.where(lane == 127, 0.0, pltpu.roll(wide, 1023, 1))
            target[before_row:before_row + 128, at] = before.astype(jnp.bfloat16)
            target[after_row:after_row + 128, at] = after.astype(jnp.bfloat16)
            return carry
        lax.fori_loop(0, count, plane, 0)

    for d in range(4):
        xs[128:256, 1024 * (d + 1):1024 * (d + 2)] = vol_ref[:, d].reshape(128, 1024)
    start_rims(vol_up, vol_down)
    start_rims(cot_up, cot_down)
    for t in range(27):
        a, b, c = t // 9, (t // 3) % 3, t % 3
        wf_ref[a, 128 * b:128 * b + 128, 128 * c:128 * c + 128] = jnp.transpose(w_ref[t])
    spread(xs, 1, 4, 1, 0, 256)

    def copy(stage, q, source, target, device):
        return pltpu.make_async_remote_copy(
            src_ref=source, dst_ref=target, send_sem=s_sem.at[stage, q],
            recv_sem=r_sem.at[stage, q], device_id=device, device_id_type=MESH)

    def rows(start, size):
        return pl.ds(pl.multiple_of(start, 8), size)

    near_first = (False, True, True, False, True, False)
    bit1, dev1 = [z0 if n else y for n in near_first], [to_n if n else to_y for n in near_first]
    bit2, dev2 = [y if n else z0 for n in near_first], [to_y if n else to_n for n in near_first]
    h1, h2, h3 = [r // 2 for r in PIECE_ROWS], [r // 4 for r in PIECE_ROWS], [r // 8 for r in PIECE_ROWS]
    k1 = [PIECE_START[q] + bit1[q] * h1[q] for q in range(6)]
    k2 = [k1[q] + bit2[q] * h2[q] for q in range(6)]
    k3 = [k2[q] + z1 * h3[q] for q in range(6)]
    o1 = [PIECE_START[q] + (1 - bit1[q]) * h1[q] for q in range(6)]
    o2 = [k1[q] + (1 - bit2[q]) * h2[q] for q in range(6)]
    o3 = [k2[q] + (1 - z1) * h3[q] for q in range(6)]

    def rows16(start, size):
        return pl.ds(pl.multiple_of(start, 16), size)

    def coded(buf, q, size):
        return buf.at[q, 0:size + 16]

    cy = [copy(0, q, coded(e_y, q, h1[q]), coded(r_y, q, h1[q]), dev1[q]) for q in range(6)]
    cn = [copy(1, q, coded(e_n, q, h2[q]), coded(r_n, q, h2[q]), dev2[q]) for q in range(6)]
    cf = [copy(2, q, coded(e_f, q, h3[q]), coded(r_f, q, h3[q]), to_f) for q in range(6)]
    gf = [copy(3, q, kgb.at[rows16(k3[q], h3[q])], kgb.at[rows16(k3[q], h3[q])], to_f) for q in range(6)]
    gn = [copy(4, q, kgb.at[rows16(k2[q], h2[q])], kgb.at[rows16(k2[q], h2[q])], dev2[q]) for q in range(6)]
    gy = [copy(5, q, kgb.at[rows16(k1[q], h1[q])], kgb.at[rows16(k1[q], h1[q])], dev1[q]) for q in range(6)]

    def post(buf, q, start, size):
        scale = s_kg[q]
        double = scale.astype(jnp.bfloat16)
        buf[q, 0:16] = jnp.concatenate([double, double], axis=0)
        buf[q, 16:16 + size] = encode(tiles(part[rows(start, size)]), scale, KG_POWER).reshape(size, 128)

    def fetch(buf, q, start, size):
        scale = buf[q, 0:16].astype(jnp.float32)[0:8]
        got = decode(buf[q, 16:16 + size].reshape(size, 128), 1.0, KG_POWER)
        part[rows(start, size)] += (tiles(got) * scale).reshape(size, 128)
        s_kg[q] = code_scale(s_kg[q] + scale).astype(jnp.float32)

    def start_y(q):
        whole = tiles(part[PIECE_START[q]:PIECE_START[q] + PIECE_ROWS[q]])
        s_kg[q] = code_scale(jnp.max(jnp.abs(whole), axis=0)).astype(jnp.float32)
        post(e_y, q, o1[q], h1[q])
        cy[q].start()

    def got_y(q):
        cy[q].wait_recv()
        fetch(r_y, q, k1[q], h1[q])
        post(e_n, q, o2[q], h2[q])
        cn[q].start()

    def got_n(q):
        cn[q].wait_recv()
        fetch(r_n, q, k2[q], h2[q])
        post(e_f, q, o3[q], h3[q])
        cf[q].start()

    def got_f(q):
        cf[q].wait_recv()
        fetch(r_f, q, k3[q], h3[q])
        kgb[rows16(k3[q], h3[q])] = encode(tiles(part[rows(k3[q], h3[q])]), s_kg[q], KG_POWER).reshape(h3[q], 128)
        gf[q].start()

    def got_gf(q):
        gf[q].wait_recv()
        gn[q].start()

    def got_gn(q):
        gn[q].wait_recv()
        gy[q].start()

    def finish_kg(q):
        gy[q].wait_recv()
        at = slice(PIECE_START[q], PIECE_START[q] + PIECE_ROWS[q])
        kg_ref[at] = (tiles(decode(kgb[at], 1.0, KG_POWER)) * (s_kg[q] * factor)).reshape(PIECE_ROWS[q], 128)

    def exchange(d, out, landing, send, recv, mine, device):
        other = pl.ds(pl.multiple_of((1 - mine) * 512, 512), 512)
        return pltpu.make_async_remote_copy(
            src_ref=out.at[d, :, other], dst_ref=landing.at[d], send_sem=send.at[d],
            recv_sem=recv.at[d], device_id=device, device_id_type=MESH)

    def fwd(d):
        return pltpu.make_async_remote_copy(
            src_ref=a_send.at[d], dst_ref=a_in.at[d], send_sem=fs_sem.at[d],
            recv_sem=fr_sem.at[d], device_id=to_col, device_id_type=MESH)

    def code_act(d):
        theirs = a_out[d, :, pl.ds(pl.multiple_of((1 - col) * 512, 512), 512)]
        blocks = [tiles(theirs[:, 128 * j:128 * j + 128]) for j in range(4)]
        peaks = [jnp.max(jnp.abs(b), axis=0) for b in blocks]
        double = code_scale(jnp.maximum(jnp.maximum(peaks[0], peaks[1]), jnp.maximum(peaks[2], peaks[3])))
        scale = double.astype(jnp.float32)
        a_send[d, 0:16] = jnp.concatenate([double, double], axis=0)
        for j in range(4):
            a_send[d, 16 + 128 * j:144 + 128 * j] = encode(blocks[j], scale, ACT_POWER).reshape(128, 128)

    def bwd(d):
        return exchange(d, b_out, b_in, bs_sem, br_sem, af, to_af)

    def conv(first, step, weights, stacked, flip, out, copy_of, before_copy=lambda d: None):
        def plane(i, carry):
            d = first + i * step
            rows_out = None
            for a in range(3):
                p = d + 2 - a if flip else d + a
                term = jnp.dot(weights[a], stacked[:, plane_at(p)], preferred_element_type=jnp.float32)
                rows_out = term if rows_out is None else rows_out + term
            up, same, down = rows_out[0:128], rows_out[128:256], rows_out[256:384]
            if flip:
                up, down = down, up
            zero = jnp.zeros((128, 128), jnp.float32)
            out[d] = (same + jnp.concatenate([zero, up[:, :896]], axis=1)
                      + jnp.concatenate([down[:, 128:], zero], axis=1))
            before_copy(d)
            copy_of(d).start()
            return carry
        lax.fori_loop(0, 2, plane, 0)

    def weight_grad(q):
        total = lax.fori_loop(
            0, 4,
            lambda d, t: t + lax.dot_general(
                xs[:, plane_at(d + q)], gb[:, plane_at(d)],
                (((1,), (1,)), ((), ())), preferred_element_type=jnp.float32),
            jnp.zeros((384, 384), jnp.float32))
        for b in range(3):
            part[q * TAP_ROWS + b * 384:q * TAP_ROWS + b * 384 + 384] = total[:, 128 * b:128 * b + 128]
        start_y(2 * q)
        start_y(2 * q + 1)

    conv(1, 1, wf_ref, xs, False, a_out, fwd, code_act)
    cot_copy.wait()
    for d in range(4):
        for rows_ref, half in ((cot_ref, col), (cot_in, 1 - col)):
            at = pl.ds(pl.multiple_of((d + 1) * 1024 + half * 512, 512), 512)
            gs[128:256, at] = rows_ref[:, d].reshape(128, 512)
    edge = jnp.zeros((128, 128), jnp.bfloat16)
    for d in range(4):
        base = 1024 * d
        inner = 1024 * (d + 1)
        gb[0:128, base:base + 896] = gs[128:256, inner + 128:inner + 1024]
        gb[0:128, base + 896:base + 1024] = edge
        gb[128:256, base:base + 1024] = gs[128:256, inner:inner + 1024]
        gb[256:384, base:base + 128] = edge
        gb[256:384, base + 128:base + 1024] = gs[128:256, inner:inner + 896]
    relay_rims(vol_up, vol_down, vol_pass)
    weight_grad(1)
    relay_rims(cot_up, cot_down, cot_pass)
    finish_rims(vol_up, vol_down, vol_pass)
    clear_edges(xs)
    spread(xs, 0, 2, 5, 0, 256)
    weight_grad(0)
    weight_grad(2)
    got_y(2)
    got_y(3)
    conv(0, 3, wf_ref, xs, False, a_out, fwd, code_act)
    got_y(0)
    got_y(1)
    got_n(2)
    got_n(3)
    for t in range(27):
        a, b, c = t // 9, (t // 3) % 3, t % 3
        wb_ref[a, 128 * b:128 * b + 128, 128 * c:128 * c + 128] = w_ref[t]
    spread(gs, 1, 4, 1, 256, 0)
    got_y(4)
    got_y(5)
    got_n(0)
    got_n(1)
    got_f(2)
    got_f(3)
    conv(1, 1, wb_ref, gs, True, b_out, bwd)
    got_n(4)
    got_n(5)
    got_f(0)
    got_f(1)
    got_gf(2)
    got_gf(3)
    finish_rims(cot_up, cot_down, cot_pass)
    for i, (plane, there) in enumerate(((0, low), (5, high))):
        @pl.when(there)
        def _():
            for rows_ref, side in ((rim_own, col), (rim_other, 1 - col)):
                at = pl.ds(pl.multiple_of(plane * 1024 + side * 512, 512), 512)
                gs[128:256, at] = rows_ref[i].reshape(128, 512)
    clear_edges(gs)
    spread(gs, 0, 2, 5, 256, 0)
    conv(0, 3, wb_ref, gs, True, b_out, bwd)
    got_f(4)
    got_f(5)
    got_gf(0)
    got_gf(1)
    got_gn(2)
    got_gn(3)
    got_gf(4)
    got_gf(5)
    got_gn(0)
    got_gn(1)
    got_gn(4)
    got_gn(5)

    for d in range(4):
        bwd(d).wait()
        own = pl.ds(pl.multiple_of(af * 512, 512), 512)
        vgrad_ref[:, d] = (b_out[d, :, own] + b_in[d]).astype(jnp.bfloat16).reshape(128, 4, 128)
    for d in range(4):
        fwd(d).wait()
        scale = a_in[d, 0:16].astype(jnp.float32)[0:8]
        got = [(tiles(decode(a_in[d, 16 + 128 * j:144 + 128 * j], 1.0, ACT_POWER)) * scale).reshape(128, 128)
               for j in range(4)]
        own = pl.ds(pl.multiple_of(col * 512, 512), 512)
        act_ref[:, d] = (a_out[d, :, own] + jnp.concatenate(got, axis=1)).astype(jnp.bfloat16).reshape(128, 4, 128)
    for q in range(6):
        finish_kg(q)
    for group in (cy, cn, cf, gf, gn, gy):
        for q in range(6):
            group[q].wait_send()


def hand_over(*refs):
    sources, targets, stages, in_sem, out_sem = refs[0:3], refs[3:6], refs[6:9], refs[9], refs[10]
    inward = [pltpu.make_async_copy(sources[i], stages[i], in_sem.at[i]) for i in range(3)]
    outward = [pltpu.make_async_copy(stages[i], targets[i], out_sem.at[i]) for i in range(3)]
    for c in inward:
        c.start()
    for i in range(3):
        inward[i].wait()
        outward[i].start()
    for c in outward:
        c.wait()


def per_device_fused(scan_volume, conv_kernel, out_cotangent):
    factor = float(4 * lax.axis_size("sa") * 8 * 128) ** (-0.5)
    f32, bf16 = jnp.float32, jnp.bfloat16
    vmem = pl.BlockSpec(memory_space=pltpu.VMEM)
    act, vgrad, kg = pl.pallas_call(
        functools.partial(fused_kernel, factor),
        out_shape=(jax.ShapeDtypeStruct((128, 4, 4, 128), bf16), jax.ShapeDtypeStruct((128, 4, 4, 128), bf16),
                   jax.ShapeDtypeStruct((3456, 128), f32)),
        in_specs=[vmem] * 3,
        out_specs=(vmem,) * 3,
        scratch_shapes=[
            pltpu.VMEM((128, 4, 4, 128), bf16), pltpu.VMEM((2, 128, 4, 128), bf16),
            pltpu.VMEM((2, 128, 4, 128), bf16), pltpu.VMEM((3, 384, 384), bf16), pltpu.VMEM((3, 384, 384), bf16),
            pltpu.VMEM((384, 6144), bf16), pltpu.VMEM((384, 6144), bf16), pltpu.VMEM((384, 4096), bf16),
            pltpu.VMEM((3456, 128), f32), pltpu.VMEM((3456, 128), bf16),
            pltpu.VMEM((6, 336, 128), bf16), pltpu.VMEM((6, 176, 128), bf16), pltpu.VMEM((6, 96, 128), bf16),
            pltpu.VMEM((6, 336, 128), bf16), pltpu.VMEM((6, 176, 128), bf16), pltpu.VMEM((6, 96, 128), bf16),
            pltpu.VMEM((6, 8, 128), f32),
            pltpu.VMEM((4, 128, 1024), f32), pltpu.VMEM((4, 528, 128), bf16), pltpu.VMEM((4, 528, 128), bf16),
            pltpu.VMEM((4, 128, 1024), f32), pltpu.VMEM((4, 128, 512), f32),
            pltpu.SemaphoreType.DMA((6, 6)), pltpu.SemaphoreType.DMA((6, 6)),
            pltpu.SemaphoreType.DMA((4,)), pltpu.SemaphoreType.DMA((4,)),
            pltpu.SemaphoreType.DMA((4,)), pltpu.SemaphoreType.DMA((4,)),
            pltpu.SemaphoreType.DMA, pltpu.SemaphoreType.DMA,
            pltpu.SemaphoreType.DMA((8,)), pltpu.SemaphoreType.DMA((8,)),
        ],
        compiler_params=pltpu.CompilerParams(
            collective_id=0, has_side_effects=True, vmem_limit_bytes=56 << 20),
    )(scan_volume, out_cotangent, conv_kernel)
    results = (act, vgrad, kg.reshape(27, 128, 128))
    anywhere = pl.BlockSpec(memory_space=pl.ANY)
    return pl.pallas_call(
        hand_over,
        out_shape=tuple(jax.ShapeDtypeStruct(r.shape, r.dtype) for r in results),
        in_specs=[anywhere] * 3,
        out_specs=(anywhere,) * 3,
        scratch_shapes=[pltpu.VMEM(r.shape, r.dtype) for r in results]
        + [pltpu.SemaphoreType.DMA((3,)), pltpu.SemaphoreType.DMA((3,))],
    )(*results)


def solution(mesh):
    sizes = (mesh.shape["sa"], mesh.shape["col"], mesh.shape["af"])
    body = per_device_fused if sizes == (8, 2, 2) else per_device
    return jax.shard_map(
        body,
        mesh=mesh,
        in_specs=(P("col", "sa", None, None), P(None, "col", "af"), P("af", "sa", "col", None)),
        out_specs=(P("af", "sa", "col", None), P("col", "sa", "af", None), P(None, "col", "af")),
        check_vma=False,
    )
```

```python
import functools

import jax
import jax.numpy as jnp
from jax import lax
from jax.experimental import pallas as pl
from jax.experimental.pallas import tpu as pltpu
from jax.sharding import PartitionSpec as P


def extended(value, sides, width):
    for axis, dim in sides:
        size, length = (lax.axis_size(axis), value.shape[dim])
        up = [(i, (i + 1) % size) for i in range(size - 1)]
        down = [(j, i) for i, j in up]
        last = lax.slice_in_dim(value, length - width, length, axis=dim)
        first = lax.slice_in_dim(value, 0, width, axis=dim)
        before = lax.ppermute(last, axis, up)
        after = lax.ppermute(first, axis, down)
        value = jnp.concatenate([before, value, after], axis=dim)
    return value


def forward_taps(padded, kernel_block, slab_depth, slab_rows, slab_width):
    channels = padded.shape[0]
    filters = kernel_block.shape[2]
    accumulated = jnp.zeros((filters, slab_depth, slab_rows, slab_width), jnp.float32)
    for depth_step in range(3):
        shifted = jnp.concatenate(
            [
                padded[
                    :,
                    depth_step : depth_step + slab_depth,
                    row_step : row_step + slab_rows,
                    col_step : col_step + slab_width,
                ]
                for row_step in range(3)
                for col_step in range(3)
            ],
            axis=0,
        )
        matrix = kernel_block[9 * depth_step : 9 * depth_step + 9].reshape(9 * channels, filters)
        accumulated = accumulated + jnp.einsum(
            "kf,kdhw->fdhw", matrix, shifted, preferred_element_type=jnp.float32
        )
    return accumulated


def backward_taps(grad_pad, kernel_block, slab_depth, slab_rows, slab_width):
    channels = kernel_block.shape[1]
    filters = kernel_block.shape[2]
    accumulated = jnp.zeros((channels, slab_depth, slab_rows, slab_width), jnp.float32)
    for depth_step in range(3):
        shifted = jnp.concatenate(
            [
                grad_pad[
                    :,
                    2 - depth_step : 2 - depth_step + slab_depth,
                    2 - row_step : 2 - row_step + slab_rows,
                    2 - col_step : 2 - col_step + slab_width,
                ]
                for row_step in range(3)
                for col_step in range(3)
            ],
            axis=0,
        )
        matrix = jnp.swapaxes(kernel_block[9 * depth_step : 9 * depth_step + 9], 1, 2).reshape(
            9 * filters, channels
        )
        accumulated = accumulated + jnp.einsum(
            "kc,kdhw->cdhw", matrix, shifted, preferred_element_type=jnp.float32
        )
    return accumulated


def weight_taps(padded, grad_slab, slab_depth, slab_rows, slab_width):
    channels = padded.shape[0]
    filters = grad_slab.shape[0]
    pieces = []
    for depth_step in range(3):
        shifted = jnp.concatenate(
            [
                padded[
                    :,
                    depth_step : depth_step + slab_depth,
                    row_step : row_step + slab_rows,
                    col_step : col_step + slab_width,
                ]
                for row_step in range(3)
                for col_step in range(3)
            ],
            axis=0,
        )
        product = jnp.einsum(
            "kdhw,fdhw->kf", shifted, grad_slab, preferred_element_type=jnp.float32
        )
        pieces.append(product.reshape(9, channels, filters))
    return jnp.concatenate(pieces, axis=0)


def per_device(scan_volume, conv_kernel, out_cotangent):
    slab_depth = scan_volume.shape[1]
    slab_rows = scan_volume.shape[2]
    slab_width = scan_volume.shape[3]
    with_rim = extended(scan_volume, (("sa", 1),), 1)
    padded_vol = jnp.pad(with_rim, ((0, 0), (0, 0), (1, 1), (1, 1)))
    partial_out = forward_taps(padded_vol, conv_kernel, slab_depth, slab_rows, slab_width)
    summed = lax.psum_scatter(partial_out, "col", scatter_dimension=2, tiled=True)
    activation = summed.astype(jnp.bfloat16)
    grad_slab = lax.all_gather(out_cotangent, "col", axis=2, tiled=True)
    grad_rim = extended(grad_slab, (("sa", 1),), 1)
    grad_pad = jnp.pad(grad_rim, ((0, 0), (0, 0), (1, 1), (1, 1)))
    volume_partial = backward_taps(grad_pad, conv_kernel, slab_depth, slab_rows, slab_width)
    volume_grad = lax.psum_scatter(volume_partial, "af", scatter_dimension=2, tiled=True).astype(
        jnp.bfloat16
    )
    weight_partial = weight_taps(padded_vol, grad_slab, slab_depth, slab_rows, slab_width)
    factor = float(slab_depth * lax.axis_size("sa") * slab_rows * slab_width) ** (-0.5)
    kernel_grad = lax.psum(weight_partial, "sa") * factor
    return (activation, volume_grad, kernel_grad)


MESH = pl.DeviceIdType.MESH
KG_POWER, ACT_POWER = 9, 17
TOP = 124.0
NEAR_FIRST = (True, False, False, False, True, True)


def code_scale(peak):
    return jnp.maximum(peak, 2.0 ** -90).astype(jnp.bfloat16)


def encode(value, scale, power):
    x = value * ((2.0 ** (TOP / power)) / scale)
    x2 = x * x
    x4 = x2 * x2
    x8 = x4 * x4
    high = x8 if power == 9 else x8 * x8
    return (high * x).astype(jnp.bfloat16)


def decode(code, scale, power):
    wide = code.astype(jnp.float32)
    size = jnp.exp2(jnp.log(jnp.abs(wide)) * (1.0 / (power * 0.6931471805599453)))
    size = jnp.where(wide == 0.0, 0.0, size) * (scale * (2.0 ** (-TOP / power)))
    return jnp.where(wide < 0.0, -size, size)


def tiles(value):
    return value.reshape(value.shape[0] // 8, 8, 128)


def fused_kernel(factor, vol_hbm, cot_hbm, w_hbm, act_ref, vgrad_ref, kg_ref,
                 vol_ref, cot_ref, w_ref, cot_in, rim_own, rim_other, wf_ref, wb_ref, xs, gs, gb,
                 part, kgb, e_y, e_n, e_f, r_y, r_n, r_f, s_kg, a_out, a_send, a_in, b_out, b_in,
                 in_sem, s_sem, r_sem, fs_sem, fr_sem, bs_sem, br_sem, cs_sem, cr_sem, hs_sem, hr_sem):
    sa = lax.axis_index("sa")
    col = lax.axis_index("col")
    af = lax.axis_index("af")
    y, z0, z1 = sa % 2, (sa // 2) % 2, sa // 4
    to_y = (sa + 1 - 2 * y, col, af)
    to_n = (sa + 2 - 4 * z0, col, af)
    to_f = (sa + 4 - 8 * z1, col, af)
    to_col = (sa, 1 - col, af)
    to_af = (sa, col, 1 - af)

    low, high = sa > 0, sa < 7
    diagonal = sa - 1 + 2 * y
    has_diagonal = jnp.logical_and(diagonal >= 0, diagonal <= 7)

    barrier = pltpu.get_barrier_semaphore()
    for device in (to_y, to_n, to_f, to_col, to_af):
        pl.semaphore_signal(barrier, inc=1, device_id=device, device_id_type=MESH)

    @pl.when(has_diagonal)
    def _():
        pl.semaphore_signal(barrier, inc=1, device_id=(diagonal, col, af), device_id_type=MESH)

    fetch_vol = pltpu.make_async_copy(vol_hbm, vol_ref, in_sem.at[0])
    fetch_w = pltpu.make_async_copy(w_hbm, w_ref, in_sem.at[1])
    fetch_cot = pltpu.make_async_copy(cot_hbm, cot_ref, in_sem.at[2])
    fetch_vol.start()
    fetch_w.start()
    fetch_cot.start()
    pl.semaphore_wait(barrier, 5 + has_diagonal.astype(jnp.int32))

    cot_copy = [pltpu.make_async_remote_copy(
        src_ref=cot_hbm.at[64 * h:64 * h + 64], dst_ref=cot_in.at[64 * h:64 * h + 64],
        send_sem=cs_sem.at[h], recv_sem=cr_sem.at[h],
        device_id=to_col, device_id_type=MESH) for h in range(2)]
    cot_copy[0].start()
    cot_copy[1].start()

    def plane_at(p):
        return slice(p * 1024, p * 1024 + 1024)

    def send(which, source, target, device):
        return pltpu.make_async_remote_copy(
            src_ref=source, dst_ref=target, send_sem=hs_sem.at[which], recv_sem=hr_sem.at[which],
            device_id=device, device_id_type=MESH)

    above, below = (sa + 1, col, af), (sa - 1, col, af)
    half = pl.ds(pl.multiple_of(128 + af * 64, 64), 64)
    vol_up = send(0, xs.at[half, 4096:5120], xs.at[half, 0:1024], above)
    vol_down = send(1, xs.at[half, 1024:2048], xs.at[half, 5120:6144], below)
    vol_pass = (send(2, xs.at[half, 0:1024], xs.at[half, 0:1024], to_af),
                send(3, xs.at[half, 5120:6144], xs.at[half, 5120:6144], to_af))
    cot_up = send(4, cot_hbm.at[:, 3], rim_own.at[0], above)
    cot_down = send(5, cot_hbm.at[:, 0], rim_own.at[1], below)
    cot_pass = (send(6, rim_own.at[0], rim_other.at[0], to_col),
                send(7, rim_own.at[1], rim_other.at[1], to_col))

    def start_rims(up, down):
        pl.when(high)(up.start)
        pl.when(low)(down.start)

    def relay_rims(up, down, onward):
        @pl.when(low)
        def _():
            up.wait_recv()
            onward[0].start()

        @pl.when(high)
        def _():
            down.wait_recv()
            onward[1].start()

    def finish_rims(up, down, onward):
        pl.when(high)(up.wait_send)
        pl.when(low)(down.wait_send)
        pl.when(low)(onward[0].wait)
        pl.when(high)(onward[1].wait)

    def clear_edges(stacked):
        @pl.when(sa == 0)
        def _():
            stacked[128:256, 0:1024] = jnp.zeros((128, 1024), jnp.bfloat16)

        @pl.when(sa == 7)
        def _():
            stacked[128:256, 5120:6144] = jnp.zeros((128, 1024), jnp.bfloat16)

    lane = lax.broadcasted_iota(jnp.int32, (128, 1024), 1) % 128

    def spread(target, first, count, step, before_row, after_row):
        def plane(i, carry):
            at = pl.ds(pl.multiple_of((first + i * step) * 1024, 1024), 1024)
            wide = target[128:256, at].astype(jnp.float32)
            before = jnp.where(lane == 0, 0.0, pltpu.roll(wide, 1, 1))
            after = jnp.where(lane == 127, 0.0, pltpu.roll(wide, 1023, 1))
            target[before_row:before_row + 128, at] = before.astype(jnp.bfloat16)
            target[after_row:after_row + 128, at] = after.astype(jnp.bfloat16)
            return carry
        lax.fori_loop(0, count, plane, 0)

    def copy(stage, q, source, target, device):
        return pltpu.make_async_remote_copy(
            src_ref=source, dst_ref=target, send_sem=s_sem.at[stage, q],
            recv_sem=r_sem.at[stage, q], device_id=device, device_id_type=MESH)

    bit1, dev1 = [z0 if n else y for n in NEAR_FIRST], [to_n if n else to_y for n in NEAR_FIRST]
    bit2, dev2 = [y if n else z0 for n in NEAR_FIRST], [to_y if n else to_n for n in NEAR_FIRST]
    k1 = [72 * q + bit1[q] * 36 for q in range(6)]
    k2 = [k1[q] + bit2[q] * 18 for q in range(6)]
    k3 = [k2[q] + z1 * 9 for q in range(6)]
    o1 = [72 * q + (1 - bit1[q]) * 36 for q in range(6)]
    o2 = [k1[q] + (1 - bit2[q]) * 18 for q in range(6)]
    o3 = [k2[q] + (1 - z1) * 9 for q in range(6)]
    cy = [copy(0, q, e_y.at[q], r_y.at[q], dev1[q]) for q in range(6)]
    cn = [copy(1, q, e_n.at[q], r_n.at[q], dev2[q]) for q in range(6)]
    cf = [copy(2, q, e_f.at[q], r_f.at[q], to_f) for q in range(6)]
    gf = [copy(3, q, kgb.at[pl.ds(k3[q], 9)], kgb.at[pl.ds(k3[q], 9)], to_f) for q in range(6)]
    gn = [copy(4, q, kgb.at[pl.ds(k2[q], 18)], kgb.at[pl.ds(k2[q], 18)], dev2[q]) for q in range(6)]
    gy = [copy(5, q, kgb.at[pl.ds(k1[q], 36)], kgb.at[pl.ds(k1[q], 36)], dev1[q]) for q in range(6)]

    def post(buf, q, start, size):
        scale = s_kg[q]
        buf[q, 0] = scale.astype(jnp.bfloat16)
        buf[q, 1:1 + size] = encode(part[pl.ds(start, size)], scale, KG_POWER)

    def fetch(buf, q, start, size):
        scale = buf[q, 0].astype(jnp.float32)
        part[pl.ds(start, size)] += decode(buf[q, 1:1 + size], scale, KG_POWER)
        s_kg[q] = code_scale(s_kg[q] + scale).astype(jnp.float32)

    def got_y(q):
        cy[q].wait_recv()
        fetch(r_y, q, k1[q], 36)
        post(e_n, q, o2[q], 18)
        cn[q].start()

    def got_n(q):
        cn[q].wait_recv()
        fetch(r_n, q, k2[q], 18)
        post(e_f, q, o3[q], 9)
        cf[q].start()

    def got_f(q):
        cf[q].wait_recv()
        fetch(r_f, q, k3[q], 9)
        kgb[pl.ds(k3[q], 9)] = encode(part[pl.ds(k3[q], 9)], s_kg[q], KG_POWER)
        gf[q].start()

    def got_gf(q):
        gf[q].wait_recv()
        gn[q].start()

    def got_gn(q):
        gn[q].wait_recv()
        gy[q].start()

    low_lanes = lax.broadcasted_iota(jnp.int32, (384, 128), 1) < 64

    def finish_kg(q):
        gy[q].wait_recv()
        gy[q + 3].wait_recv()
        first = decode(kgb[72 * q:72 * q + 72], s_kg[q] * factor, KG_POWER).reshape(576, 128)
        second = decode(kgb[72 * q + 216:72 * q + 288], s_kg[q + 3] * factor, KG_POWER).reshape(576, 128)
        straight = jnp.where(low_lanes, first[0:384], second[0:384])
        crossed = pltpu.roll(jnp.where(low_lanes, second[0:384], first[0:384]), 64, 1)
        base = 1152 * q
        kg_ref[base:base + 384] = straight
        kg_ref[base + 384:base + 768] = crossed
        few = low_lanes[0:192]
        kg_ref[base + 768:base + 960] = jnp.where(few, first[384:576], second[384:576])
        kg_ref[base + 960:base + 1152] = pltpu.roll(jnp.where(few, second[384:576], first[384:576]), 64, 1)

    def weight_grad(h, q):
        total = lax.dot_general(
            xs[:, 1024 * q:1024 * q + 4096], gb[192 * h:192 * h + 192, :],
            (((1,), (1,)), ((), ())), preferred_element_type=jnp.float32)
        at, piece = 72 * (3 * h + q), 3 * h + q
        parts = [total[0:192, 128:192], total[192:384, 128:192]]
        packed = jnp.concatenate(parts if h == 0 else parts[::-1], axis=1)
        part[at:at + 48] = tiles(total[:, 0:128])
        part[at + 48:at + 72] = tiles(packed)
        s_kg[piece] = code_scale(jnp.max(jnp.abs(part[at:at + 72]), axis=0)).astype(jnp.float32)
        post(e_y, piece, o1[piece], 36)
        cy[piece].start()

    def fwd(d):
        return pltpu.make_async_remote_copy(
            src_ref=a_send.at[d], dst_ref=a_in.at[d], send_sem=fs_sem.at[d],
            recv_sem=fr_sem.at[d], device_id=to_col, device_id_type=MESH)

    def bwd(d):
        return pltpu.make_async_remote_copy(
            src_ref=b_out.at[d, :, pl.ds(pl.multiple_of((1 - af) * 512, 512), 512)], dst_ref=b_in.at[d],
            send_sem=bs_sem.at[d], recv_sem=br_sem.at[d], device_id=to_af, device_id_type=MESH)

    def code_act(d):
        theirs = a_out[d, :, pl.ds(pl.multiple_of((1 - col) * 512, 512), 512)]
        blocks = [tiles(theirs[:, 128 * j:128 * j + 128]) for j in range(4)]
        peaks = [jnp.max(jnp.abs(b), axis=0) for b in blocks]
        short = code_scale(jnp.maximum(jnp.maximum(peaks[0], peaks[1]), jnp.maximum(peaks[2], peaks[3])))
        scale = short.astype(jnp.float32)
        a_send[d, 0] = short
        for j in range(4):
            a_send[d, 1 + 16 * j:17 + 16 * j] = encode(blocks[j], scale, ACT_POWER)

    def finish_act(d):
        fwd(d).wait_recv()
        scale = a_in[d, 0].astype(jnp.float32)
        got = [decode(a_in[d, 1 + 16 * j:17 + 16 * j], scale, ACT_POWER).reshape(128, 128) for j in range(4)]
        own = pl.ds(pl.multiple_of(col * 512, 512), 512)
        act_ref[:, d] = (a_out[d, :, own] + jnp.concatenate(got, axis=1)).astype(jnp.bfloat16).reshape(128, 4, 128)

    def finish_bwd(d):
        bwd(d).wait_recv()
        own = pl.ds(pl.multiple_of(af * 512, 512), 512)
        vgrad_ref[:, d] = (b_out[d, :, own] + b_in[d]).astype(jnp.bfloat16).reshape(128, 4, 128)

    def conv(d, weights, stacked, flip, out):
        tall = jnp.concatenate([stacked[:, plane_at(d + 2 - a if flip else d + a)] for a in range(3)], axis=0)
        rows_out = jnp.dot(weights[...], tall, preferred_element_type=jnp.float32)
        up, same, down = rows_out[0:128], rows_out[128:256], rows_out[256:384]
        if flip:
            up, down = down, up
        zero = jnp.zeros((128, 128), jnp.float32)
        out[d] = (same + jnp.concatenate([zero, up[:, :896]], axis=1)
                  + jnp.concatenate([down[:, 128:], zero], axis=1))

    def forward(d):
        conv(d, wf_ref, xs, False, a_out)
        code_act(d)

    def backward(d):
        conv(d, wb_ref, gs, True, b_out)
        bwd(d).start()

    def place_cot(h):
        f0, edge = 64 * h, jnp.zeros((64, 128), jnp.bfloat16)
        for d in range(4):
            for rows_ref, side in ((cot_ref, col), (cot_in, 1 - col)):
                at = pl.ds(pl.multiple_of((d + 1) * 1024 + side * 512, 512), 512)
                gs[128 + f0:192 + f0, at] = rows_ref[f0:f0 + 64, d].reshape(64, 512)
        slots = (0, 64, 128) if h == 0 else (64, 0, 128)
        for d in range(4):
            base, inner = 1024 * d, 1024 * (d + 1)
            mine = slice(128 + f0, 192 + f0)
            r0, r1, r2 = [slice(192 * h + s, 192 * h + s + 64) for s in slots]
            gb[r0, base:base + 896] = gs[mine, inner + 128:inner + 1024]
            gb[r0, base + 896:base + 1024] = edge
            gb[r1, base:base + 1024] = gs[mine, inner:inner + 1024]
            gb[r2, base:base + 128] = edge
            gb[r2, base + 128:base + 1024] = gs[mine, inner:inner + 896]

    def prepare_volume():
        fetch_vol.wait()
        for d in range(4):
            xs[128:256, 1024 * (d + 1):1024 * (d + 2)] = vol_ref[:, d].reshape(128, 1024)

    def place_weights(target, turn):
        for t in range(27):
            a, b, c = t // 9, (t // 3) % 3, t % 3
            block = jnp.transpose(w_ref[t]) if turn else w_ref[t]
            target[128 * b:128 * b + 128, 384 * a + 128 * c:384 * a + 128 * c + 128] = block

    def place_rims():
        for i, (plane, there) in enumerate(((0, low), (5, high))):
            @pl.when(there)
            def _():
                for rows_ref, side in ((rim_own, col), (rim_other, 1 - col)):
                    at = pl.ds(pl.multiple_of(plane * 1024 + side * 512, 512), 512)
                    gs[128:256, at] = rows_ref[i].reshape(128, 512)
        clear_edges(gs)

    prepare_volume()
    start_rims(vol_up, vol_down)
    start_rims(cot_up, cot_down)
    fetch_w.wait()
    place_weights(wf_ref, True)
    spread(xs, 1, 4, 1, 0, 256)
    forward(1)
    forward(2)
    place_weights(wb_ref, False)
    fetch_cot.wait()
    cot_copy[0].wait_recv()
    place_cot(0)
    weight_grad(0, 1)
    relay_rims(vol_up, vol_down, vol_pass)
    finish_rims(vol_up, vol_down, vol_pass)
    clear_edges(xs)
    spread(xs, 0, 2, 5, 0, 256)
    weight_grad(0, 0)
    weight_grad(0, 2)
    cot_copy[1].wait_recv()
    fwd(1).start()
    fwd(2).start()
    place_cot(1)
    got_y(1)
    weight_grad(1, 1)
    got_y(0)
    weight_grad(1, 0)
    got_y(2)
    got_n(1)
    weight_grad(1, 2)
    relay_rims(cot_up, cot_down, cot_pass)
    got_n(0)
    got_n(2)
    got_f(1)
    got_y(4)
    got_f(0)
    got_y(3)
    got_f(2)
    got_y(5)
    got_gf(1)
    forward(0)
    fwd(0).start()
    got_n(4)
    got_gf(0)
    got_n(3)
    got_gf(2)
    got_gn(1)
    forward(3)
    fwd(3).start()
    got_n(5)
    got_f(4)
    got_gn(0)
    spread(gs, 1, 4, 1, 256, 0)
    got_f(3)
    got_gn(2)
    backward(1)
    got_f(5)
    got_gf(4)
    backward(2)
    got_gf(3)
    finish_rims(cot_up, cot_down, cot_pass)
    place_rims()
    spread(gs, 0, 2, 5, 256, 0)
    got_gf(5)
    got_gn(4)
    backward(0)
    got_gn(3)
    got_gn(5)
    backward(3)
    for d in (1, 2, 0, 3):
        finish_bwd(d)
    for d in (1, 2, 0, 3):
        finish_act(d)
    finish_kg(1)
    finish_kg(0)
    finish_kg(2)
    for group in (cy, cn, cf, gf, gn, gy):
        for q in range(6):
            group[q].wait_send()
    for d in range(4):
        fwd(d).wait_send()
        bwd(d).wait_send()
    for h in range(2):
        cot_copy[h].wait_send()


def hand_over(*refs):
    sources, targets, sem = refs[0:3], refs[3:6], refs[6]
    copies = [pltpu.make_async_copy(sources[i], targets[i], sem.at[i]) for i in range(3)]
    for c in copies:
        c.start()
    for c in copies:
        c.wait()


def per_device_fused(scan_volume, conv_kernel, out_cotangent):
    factor = float(4 * lax.axis_size("sa") * 8 * 128) ** (-0.5)
    f32, bf16 = jnp.float32, jnp.bfloat16
    vmem = pl.BlockSpec(memory_space=pltpu.VMEM)
    act, vgrad, kg = pl.pallas_call(
        functools.partial(fused_kernel, factor),
        out_shape=(pltpu.VMEM((128, 4, 4, 128), bf16), pltpu.VMEM((128, 4, 4, 128), bf16),
                   pltpu.VMEM((3456, 128), f32)),
        in_specs=[pl.BlockSpec(memory_space=pl.ANY)] * 3,
        out_specs=(vmem,) * 3,
        scratch_shapes=[
            pltpu.VMEM((128, 4, 8, 128), bf16), pltpu.VMEM((128, 4, 4, 128), bf16), pltpu.VMEM((27, 128, 128), bf16),
            pltpu.VMEM((128, 4, 4, 128), bf16), pltpu.VMEM((2, 128, 4, 128), bf16),
            pltpu.VMEM((2, 128, 4, 128), bf16), pltpu.VMEM((384, 1152), bf16), pltpu.VMEM((384, 1152), bf16),
            pltpu.VMEM((384, 6144), bf16), pltpu.VMEM((384, 6144), bf16), pltpu.VMEM((384, 4096), bf16),
            pltpu.VMEM((432, 8, 128), f32), pltpu.VMEM((432, 8, 128), bf16),
            pltpu.VMEM((6, 37, 8, 128), bf16), pltpu.VMEM((6, 19, 8, 128), bf16), pltpu.VMEM((6, 10, 8, 128), bf16),
            pltpu.VMEM((6, 37, 8, 128), bf16), pltpu.VMEM((6, 19, 8, 128), bf16), pltpu.VMEM((6, 10, 8, 128), bf16),
            pltpu.VMEM((6, 8, 128), f32),
            pltpu.VMEM((4, 128, 1024), f32), pltpu.VMEM((4, 65, 8, 128), bf16), pltpu.VMEM((4, 65, 8, 128), bf16),
            pltpu.VMEM((4, 128, 1024), f32), pltpu.VMEM((4, 128, 512), f32),
            pltpu.SemaphoreType.DMA((3,)),
            pltpu.SemaphoreType.DMA((6, 6)), pltpu.SemaphoreType.DMA((6, 6)),
            pltpu.SemaphoreType.DMA((4,)), pltpu.SemaphoreType.DMA((4,)),
            pltpu.SemaphoreType.DMA((4,)), pltpu.SemaphoreType.DMA((4,)),
            pltpu.SemaphoreType.DMA((2,)), pltpu.SemaphoreType.DMA((2,)),
            pltpu.SemaphoreType.DMA((8,)), pltpu.SemaphoreType.DMA((8,)),
        ],
        compiler_params=pltpu.CompilerParams(
            collective_id=0, has_side_effects=True, vmem_limit_bytes=56 << 20),
    )(scan_volume, out_cotangent, conv_kernel)
    results = (act, vgrad, kg.reshape(27, 128, 128))
    anywhere = pl.BlockSpec(memory_space=pl.ANY)
    return pl.pallas_call(
        hand_over,
        out_shape=tuple(jax.ShapeDtypeStruct(r.shape, r.dtype) for r in results),
        in_specs=[vmem] * 3,
        out_specs=(anywhere,) * 3,
        scratch_shapes=[pltpu.SemaphoreType.DMA((3,))],
    )(*[pltpu.with_memory_space_constraint(r, pltpu.VMEM) for r in results])


def solution(mesh):
    sizes = (mesh.shape["sa"], mesh.shape["col"], mesh.shape["af"])
    body = per_device_fused if sizes == (8, 2, 2) else per_device
    return jax.shard_map(
        body,
        mesh=mesh,
        in_specs=(P("col", "sa", None, None), P(None, "col", "af"), P("af", "sa", "col", None)),
        out_specs=(P("af", "sa", "col", None), P("col", "sa", "af", None), P(None, "col", "af")),
        check_vma=False,
    )
```

```python
import functools

import jax
import jax.numpy as jnp
from jax import lax
from jax.experimental import pallas as pl
from jax.experimental.pallas import tpu as pltpu
from jax.sharding import PartitionSpec as P


def extended(value, sides, width):
    for axis, dim in sides:
        size, length = (lax.axis_size(axis), value.shape[dim])
        up = [(i, (i + 1) % size) for i in range(size - 1)]
        down = [(j, i) for i, j in up]
        last = lax.slice_in_dim(value, length - width, length, axis=dim)
        first = lax.slice_in_dim(value, 0, width, axis=dim)
        before = lax.ppermute(last, axis, up)
        after = lax.ppermute(first, axis, down)
        value = jnp.concatenate([before, value, after], axis=dim)
    return value


def forward_taps(padded, kernel_block, slab_depth, slab_rows, slab_width):
    channels = padded.shape[0]
    filters = kernel_block.shape[2]
    accumulated = jnp.zeros((filters, slab_depth, slab_rows, slab_width), jnp.float32)
    for depth_step in range(3):
        shifted = jnp.concatenate(
            [
                padded[
                    :,
                    depth_step : depth_step + slab_depth,
                    row_step : row_step + slab_rows,
                    col_step : col_step + slab_width,
                ]
                for row_step in range(3)
                for col_step in range(3)
            ],
            axis=0,
        )
        matrix = kernel_block[9 * depth_step : 9 * depth_step + 9].reshape(9 * channels, filters)
        accumulated = accumulated + jnp.einsum(
            "kf,kdhw->fdhw", matrix, shifted, preferred_element_type=jnp.float32
        )
    return accumulated


def backward_taps(grad_pad, kernel_block, slab_depth, slab_rows, slab_width):
    channels = kernel_block.shape[1]
    filters = kernel_block.shape[2]
    accumulated = jnp.zeros((channels, slab_depth, slab_rows, slab_width), jnp.float32)
    for depth_step in range(3):
        shifted = jnp.concatenate(
            [
                grad_pad[
                    :,
                    2 - depth_step : 2 - depth_step + slab_depth,
                    2 - row_step : 2 - row_step + slab_rows,
                    2 - col_step : 2 - col_step + slab_width,
                ]
                for row_step in range(3)
                for col_step in range(3)
            ],
            axis=0,
        )
        matrix = jnp.swapaxes(kernel_block[9 * depth_step : 9 * depth_step + 9], 1, 2).reshape(
            9 * filters, channels
        )
        accumulated = accumulated + jnp.einsum(
            "kc,kdhw->cdhw", matrix, shifted, preferred_element_type=jnp.float32
        )
    return accumulated


def weight_taps(padded, grad_slab, slab_depth, slab_rows, slab_width):
    channels = padded.shape[0]
    filters = grad_slab.shape[0]
    pieces = []
    for depth_step in range(3):
        shifted = jnp.concatenate(
            [
                padded[
                    :,
                    depth_step : depth_step + slab_depth,
                    row_step : row_step + slab_rows,
                    col_step : col_step + slab_width,
                ]
                for row_step in range(3)
                for col_step in range(3)
            ],
            axis=0,
        )
        product = jnp.einsum(
            "kdhw,fdhw->kf", shifted, grad_slab, preferred_element_type=jnp.float32
        )
        pieces.append(product.reshape(9, channels, filters))
    return jnp.concatenate(pieces, axis=0)


def per_device(scan_volume, conv_kernel, out_cotangent):
    slab_depth = scan_volume.shape[1]
    slab_rows = scan_volume.shape[2]
    slab_width = scan_volume.shape[3]
    with_rim = extended(scan_volume, (("sa", 1),), 1)
    padded_vol = jnp.pad(with_rim, ((0, 0), (0, 0), (1, 1), (1, 1)))
    partial_out = forward_taps(padded_vol, conv_kernel, slab_depth, slab_rows, slab_width)
    summed = lax.psum_scatter(partial_out, "col", scatter_dimension=2, tiled=True)
    activation = summed.astype(jnp.bfloat16)
    grad_slab = lax.all_gather(out_cotangent, "col", axis=2, tiled=True)
    grad_rim = extended(grad_slab, (("sa", 1),), 1)
    grad_pad = jnp.pad(grad_rim, ((0, 0), (0, 0), (1, 1), (1, 1)))
    volume_partial = backward_taps(grad_pad, conv_kernel, slab_depth, slab_rows, slab_width)
    volume_grad = lax.psum_scatter(volume_partial, "af", scatter_dimension=2, tiled=True).astype(
        jnp.bfloat16
    )
    weight_partial = weight_taps(padded_vol, grad_slab, slab_depth, slab_rows, slab_width)
    factor = float(slab_depth * lax.axis_size("sa") * slab_rows * slab_width) ** (-0.5)
    kernel_grad = lax.psum(weight_partial, "sa") * factor
    return (activation, volume_grad, kernel_grad)


MESH = pl.DeviceIdType.MESH
KG_POWER, ACT_POWER = 9, 17
TOP = 124.0
NEAR_FIRST = (True, False, False, False, True, True)


def code_scale(peak):
    return jnp.maximum(peak, 2.0 ** -90).astype(jnp.bfloat16)


def encode(value, scale, power):
    x = value * ((2.0 ** (TOP / power)) / scale)
    x2 = x * x
    x4 = x2 * x2
    x8 = x4 * x4
    high = x8 if power == 9 else x8 * x8
    return (high * x).astype(jnp.bfloat16)


def decode(code, scale, power):
    wide = code.astype(jnp.float32)
    size = jnp.exp2(jnp.log(jnp.abs(wide)) * (1.0 / (power * 0.6931471805599453)))
    size = jnp.where(wide == 0.0, 0.0, size) * (scale * (2.0 ** (-TOP / power)))
    return jnp.where(wide < 0.0, -size, size)


def tiles(value):
    return value.reshape(value.shape[0] // 8, 8, 128)


def fused_kernel(factor, vol_hbm, cot_hbm, w_hbm, act_ref, vgrad_ref, kg_ref,
                 vol_ref, cot_ref, w_ref, cot_in, rim_own, rim_other, wf_ref, wb_ref, xs, gs, gb,
                 part, kgb, e_y, e_n, e_f, r_y, r_n, r_f, s_kg, a_out, a_send, a_in, b_out, b_in,
                 in_sem, s_sem, r_sem, fs_sem, fr_sem, bs_sem, br_sem, cs_sem, cr_sem, hs_sem, hr_sem):
    sa = lax.axis_index("sa")
    col = lax.axis_index("col")
    af = lax.axis_index("af")
    y, z0, z1 = sa % 2, (sa // 2) % 2, sa // 4
    to_y = (sa + 1 - 2 * y, col, af)
    to_n = (sa + 2 - 4 * z0, col, af)
    to_f = (sa + 4 - 8 * z1, col, af)
    to_col = (sa, 1 - col, af)
    to_af = (sa, col, 1 - af)

    low, high = sa > 0, sa < 7
    diagonal = sa - 1 + 2 * y
    has_diagonal = jnp.logical_and(diagonal >= 0, diagonal <= 7)

    barrier = pltpu.get_barrier_semaphore()
    for device in (to_y, to_n, to_f, to_col, to_af):
        pl.semaphore_signal(barrier, inc=1, device_id=device, device_id_type=MESH)

    @pl.when(has_diagonal)
    def _():
        pl.semaphore_signal(barrier, inc=1, device_id=(diagonal, col, af), device_id_type=MESH)

    fetch_vol = pltpu.make_async_copy(vol_hbm, vol_ref, in_sem.at[0])
    fetch_w = pltpu.make_async_copy(w_hbm, w_ref, in_sem.at[1])
    fetch_cot = pltpu.make_async_copy(cot_hbm, cot_ref, in_sem.at[2])
    fetch_vol.start()
    fetch_w.start()
    fetch_cot.start()
    pl.semaphore_wait(barrier, 5 + has_diagonal.astype(jnp.int32))

    cot_copy = [pltpu.make_async_remote_copy(
        src_ref=cot_hbm.at[64 * h:64 * h + 64], dst_ref=cot_in.at[64 * h:64 * h + 64],
        send_sem=cs_sem.at[h], recv_sem=cr_sem.at[h],
        device_id=to_col, device_id_type=MESH) for h in range(2)]
    cot_copy[0].start()
    cot_copy[1].start()

    def plane_at(p):
        return slice(p * 1024, p * 1024 + 1024)

    def send(which, source, target, device):
        return pltpu.make_async_remote_copy(
            src_ref=source, dst_ref=target, send_sem=hs_sem.at[which], recv_sem=hr_sem.at[which],
            device_id=device, device_id_type=MESH)

    above, below = (sa + 1, col, af), (sa - 1, col, af)
    half = pl.ds(pl.multiple_of(128 + af * 64, 64), 64)
    vol_up = send(0, xs.at[half, 4096:5120], xs.at[half, 0:1024], above)
    vol_down = send(1, xs.at[half, 1024:2048], xs.at[half, 5120:6144], below)
    vol_pass = (send(2, xs.at[half, 0:1024], xs.at[half, 0:1024], to_af),
                send(3, xs.at[half, 5120:6144], xs.at[half, 5120:6144], to_af))
    cot_up = send(4, cot_hbm.at[:, 3], rim_own.at[0], above)
    cot_down = send(5, cot_hbm.at[:, 0], rim_own.at[1], below)
    cot_pass = (send(6, rim_own.at[0], rim_other.at[0], to_col),
                send(7, rim_own.at[1], rim_other.at[1], to_col))

    def start_rims(up, down):
        pl.when(high)(up.start)
        pl.when(low)(down.start)

    def relay_rims(up, down, onward):
        @pl.when(low)
        def _():
            up.wait_recv()
            onward[0].start()

        @pl.when(high)
        def _():
            down.wait_recv()
            onward[1].start()

    def finish_rims(up, down, onward):
        pl.when(high)(up.wait_send)
        pl.when(low)(down.wait_send)
        pl.when(low)(onward[0].wait)
        pl.when(high)(onward[1].wait)

    def clear_edges(stacked):
        @pl.when(sa == 0)
        def _():
            stacked[128:256, 0:1024] = jnp.zeros((128, 1024), jnp.bfloat16)

        @pl.when(sa == 7)
        def _():
            stacked[128:256, 5120:6144] = jnp.zeros((128, 1024), jnp.bfloat16)

    lane = lax.broadcasted_iota(jnp.int32, (128, 1024), 1) % 128

    def spread(target, first, count, step, before_row, after_row):
        def plane(i, carry):
            at = pl.ds(pl.multiple_of((first + i * step) * 1024, 1024), 1024)
            wide = target[128:256, at].astype(jnp.float32)
            before = jnp.where(lane == 0, 0.0, pltpu.roll(wide, 1, 1))
            after = jnp.where(lane == 127, 0.0, pltpu.roll(wide, 1023, 1))
            target[before_row:before_row + 128, at] = before.astype(jnp.bfloat16)
            target[after_row:after_row + 128, at] = after.astype(jnp.bfloat16)
            return carry
        lax.fori_loop(0, count, plane, 0)

    def copy(stage, q, source, target, device):
        return pltpu.make_async_remote_copy(
            src_ref=source, dst_ref=target, send_sem=s_sem.at[stage, q],
            recv_sem=r_sem.at[stage, q], device_id=device, device_id_type=MESH)

    bit1, dev1 = [z0 if n else y for n in NEAR_FIRST], [to_n if n else to_y for n in NEAR_FIRST]
    bit2, dev2 = [y if n else z0 for n in NEAR_FIRST], [to_y if n else to_n for n in NEAR_FIRST]
    k1 = [72 * q + bit1[q] * 36 for q in range(6)]
    k2 = [k1[q] + bit2[q] * 18 for q in range(6)]
    k3 = [k2[q] + z1 * 9 for q in range(6)]
    o1 = [72 * q + (1 - bit1[q]) * 36 for q in range(6)]
    o2 = [k1[q] + (1 - bit2[q]) * 18 for q in range(6)]
    o3 = [k2[q] + (1 - z1) * 9 for q in range(6)]
    cy = [copy(0, q, e_y.at[q], r_y.at[q], dev1[q]) for q in range(6)]
    cn = [copy(1, q, e_n.at[q], r_n.at[q], dev2[q]) for q in range(6)]
    cf = [copy(2, q, e_f.at[q], r_f.at[q], to_f) for q in range(6)]
    gf = [copy(3, q, kgb.at[pl.ds(k3[q], 9)], kgb.at[pl.ds(k3[q], 9)], to_f) for q in range(6)]
    gn = [copy(4, q, kgb.at[pl.ds(k2[q], 18)], kgb.at[pl.ds(k2[q], 18)], dev2[q]) for q in range(6)]
    gy = [copy(5, q, kgb.at[pl.ds(k1[q], 36)], kgb.at[pl.ds(k1[q], 36)], dev1[q]) for q in range(6)]

    def post(buf, q, start, size):
        scale = s_kg[q]
        buf[q, 0] = scale.astype(jnp.bfloat16)
        buf[q, 1:1 + size] = encode(part[pl.ds(start, size)], scale, KG_POWER)

    def fetch(buf, q, start, size):
        scale = buf[q, 0].astype(jnp.float32)
        part[pl.ds(start, size)] += decode(buf[q, 1:1 + size], scale, KG_POWER)
        s_kg[q] = code_scale(s_kg[q] + scale).astype(jnp.float32)

    def got_y(q):
        cy[q].wait_recv()
        fetch(r_y, q, k1[q], 36)
        post(e_n, q, o2[q], 18)
        cn[q].start()

    def got_n(q):
        cn[q].wait_recv()
        fetch(r_n, q, k2[q], 18)
        post(e_f, q, o3[q], 9)
        cf[q].start()

    def got_f(q):
        cf[q].wait_recv()
        fetch(r_f, q, k3[q], 9)
        kgb[pl.ds(k3[q], 9)] = encode(part[pl.ds(k3[q], 9)], s_kg[q], KG_POWER)
        gf[q].start()

    def got_gf(q):
        gf[q].wait_recv()
        gn[q].start()

    def got_gn(q):
        gn[q].wait_recv()
        gy[q].start()

    low_lanes = lax.broadcasted_iota(jnp.int32, (384, 128), 1) < 64

    def finish_kg(q):
        gy[q].wait_recv()
        gy[q + 3].wait_recv()
        first = decode(kgb[72 * q:72 * q + 72], s_kg[q] * factor, KG_POWER).reshape(576, 128)
        second = decode(kgb[72 * q + 216:72 * q + 288], s_kg[q + 3] * factor, KG_POWER).reshape(576, 128)
        straight = jnp.where(low_lanes, first[0:384], second[0:384])
        crossed = pltpu.roll(jnp.where(low_lanes, second[0:384], first[0:384]), 64, 1)
        base = 1152 * q
        kg_ref[base:base + 384] = straight
        kg_ref[base + 384:base + 768] = crossed
        few = low_lanes[0:192]
        kg_ref[base + 768:base + 960] = jnp.where(few, first[384:576], second[384:576])
        kg_ref[base + 960:base + 1152] = pltpu.roll(jnp.where(few, second[384:576], first[384:576]), 64, 1)

    def weight_grad(h, q):
        total = lax.dot_general(
            xs[:, 1024 * q:1024 * q + 4096], gb[192 * h:192 * h + 192, :],
            (((1,), (1,)), ((), ())), preferred_element_type=jnp.float32)
        at, piece = 72 * (3 * h + q), 3 * h + q
        parts = [total[0:192, 128:192], total[192:384, 128:192]]
        packed = jnp.concatenate(parts if h == 0 else parts[::-1], axis=1)
        part[at:at + 48] = tiles(total[:, 0:128])
        part[at + 48:at + 72] = tiles(packed)
        s_kg[piece] = code_scale(jnp.max(jnp.abs(part[at:at + 72]), axis=0)).astype(jnp.float32)
        post(e_y, piece, o1[piece], 36)
        cy[piece].start()

    def fwd(d):
        return pltpu.make_async_remote_copy(
            src_ref=a_send.at[d], dst_ref=a_in.at[d], send_sem=fs_sem.at[d],
            recv_sem=fr_sem.at[d], device_id=to_col, device_id_type=MESH)

    def bwd(d):
        return pltpu.make_async_remote_copy(
            src_ref=b_out.at[d, :, pl.ds(pl.multiple_of((1 - af) * 512, 512), 512)], dst_ref=b_in.at[d],
            send_sem=bs_sem.at[d], recv_sem=br_sem.at[d], device_id=to_af, device_id_type=MESH)

    def code_act(d):
        theirs = a_out[d, :, pl.ds(pl.multiple_of((1 - col) * 512, 512), 512)]
        blocks = [tiles(theirs[:, 128 * j:128 * j + 128]) for j in range(4)]
        peaks = [jnp.max(jnp.abs(b), axis=0) for b in blocks]
        short = code_scale(jnp.maximum(jnp.maximum(peaks[0], peaks[1]), jnp.maximum(peaks[2], peaks[3])))
        scale = short.astype(jnp.float32)
        a_send[d, 0] = short
        for j in range(4):
            a_send[d, 1 + 16 * j:17 + 16 * j] = encode(blocks[j], scale, ACT_POWER)

    def finish_act(d):
        fwd(d).wait_recv()
        scale = a_in[d, 0].astype(jnp.float32)
        got = [decode(a_in[d, 1 + 16 * j:17 + 16 * j], scale, ACT_POWER).reshape(128, 128) for j in range(4)]
        own = pl.ds(pl.multiple_of(col * 512, 512), 512)
        act_ref[:, d] = (a_out[d, :, own] + jnp.concatenate(got, axis=1)).astype(jnp.bfloat16).reshape(128, 4, 128)

    def finish_bwd(d):
        bwd(d).wait_recv()
        own = pl.ds(pl.multiple_of(af * 512, 512), 512)
        vgrad_ref[:, d] = (b_out[d, :, own] + b_in[d]).astype(jnp.bfloat16).reshape(128, 4, 128)

    def conv(d, weights, stacked, flip, out):
        tall = jnp.concatenate([stacked[:, plane_at(d + 2 - a if flip else d + a)] for a in range(3)], axis=0)
        rows_out = jnp.dot(weights[...], tall, preferred_element_type=jnp.float32)
        up, same, down = rows_out[0:128], rows_out[128:256], rows_out[256:384]
        if flip:
            up, down = down, up
        zero = jnp.zeros((128, 128), jnp.float32)
        out[d] = (same + jnp.concatenate([zero, up[:, :896]], axis=1)
                  + jnp.concatenate([down[:, 128:], zero], axis=1))

    def forward(d):
        conv(d, wf_ref, xs, False, a_out)
        code_act(d)

    def backward(d):
        conv(d, wb_ref, gs, True, b_out)
        bwd(d).start()

    def place_cot(h):
        f0, edge = 64 * h, jnp.zeros((64, 128), jnp.bfloat16)
        for d in range(4):
            for rows_ref, side in ((cot_ref, col), (cot_in, 1 - col)):
                at = pl.ds(pl.multiple_of((d + 1) * 1024 + side * 512, 512), 512)
                gs[128 + f0:192 + f0, at] = rows_ref[f0:f0 + 64, d].reshape(64, 512)
        slots = (0, 64, 128) if h == 0 else (64, 0, 128)
        for d in range(4):
            base, inner = 1024 * d, 1024 * (d + 1)
            mine = slice(128 + f0, 192 + f0)
            r0, r1, r2 = [slice(192 * h + s, 192 * h + s + 64) for s in slots]
            gb[r0, base:base + 896] = gs[mine, inner + 128:inner + 1024]
            gb[r0, base + 896:base + 1024] = edge
            gb[r1, base:base + 1024] = gs[mine, inner:inner + 1024]
            gb[r2, base:base + 128] = edge
            gb[r2, base + 128:base + 1024] = gs[mine, inner:inner + 896]

    def prepare_volume():
        fetch_vol.wait()
        for d in range(4):
            xs[128:256, 1024 * (d + 1):1024 * (d + 2)] = vol_ref[:, d].reshape(128, 1024)

    def place_weights(target, turn):
        for t in range(27):
            a, b, c = t // 9, (t // 3) % 3, t % 3
            block = jnp.transpose(w_ref[t]) if turn else w_ref[t]
            target[128 * b:128 * b + 128, 384 * a + 128 * c:384 * a + 128 * c + 128] = block

    def place_rims():
        for i, (plane, there) in enumerate(((0, low), (5, high))):
            @pl.when(there)
            def _():
                for rows_ref, side in ((rim_own, col), (rim_other, 1 - col)):
                    at = pl.ds(pl.multiple_of(plane * 1024 + side * 512, 512), 512)
                    gs[128:256, at] = rows_ref[i].reshape(128, 512)
        clear_edges(gs)

    prepare_volume()
    start_rims(vol_up, vol_down)
    fetch_w.wait()
    place_weights(wf_ref, True)
    spread(xs, 1, 4, 1, 0, 256)
    forward(1)
    forward(2)
    start_rims(cot_up, cot_down)
    fetch_cot.wait()
    cot_copy[0].wait_recv()
    place_cot(0)
    weight_grad(0, 1)
    relay_rims(vol_up, vol_down, vol_pass)
    finish_rims(vol_up, vol_down, vol_pass)
    clear_edges(xs)
    spread(xs, 0, 2, 5, 0, 256)
    weight_grad(0, 0)
    weight_grad(0, 2)
    cot_copy[1].wait_recv()
    fwd(1).start()
    fwd(2).start()
    place_cot(1)
    got_y(1)
    weight_grad(1, 1)
    got_y(0)
    weight_grad(1, 0)
    got_y(2)
    got_n(1)
    weight_grad(1, 2)
    relay_rims(cot_up, cot_down, cot_pass)
    got_n(0)
    got_n(2)
    got_f(1)
    got_y(4)
    got_f(0)
    got_y(3)
    got_f(2)
    got_y(5)
    got_gf(1)
    forward(0)
    fwd(0).start()
    got_n(4)
    got_gf(0)
    got_n(3)
    got_gf(2)
    got_gn(1)
    forward(3)
    fwd(3).start()
    got_n(5)
    got_f(4)
    got_gn(0)
    place_weights(wb_ref, False)
    spread(gs, 1, 4, 1, 256, 0)
    got_f(3)
    got_gn(2)
    backward(1)
    got_f(5)
    got_gf(4)
    backward(2)
    got_gf(3)
    finish_rims(cot_up, cot_down, cot_pass)
    place_rims()
    spread(gs, 0, 2, 5, 256, 0)
    finish_act(1)
    finish_act(2)
    got_gf(5)
    got_gn(4)
    finish_bwd(1)
    backward(0)
    got_gn(3)
    finish_bwd(2)
    finish_act(0)
    got_gn(5)
    backward(3)
    finish_act(3)
    finish_bwd(0)
    finish_kg(1)
    finish_kg(0)
    finish_bwd(3)
    finish_kg(2)
    for group in (cy, cn, cf, gf, gn, gy):
        for q in range(6):
            group[q].wait_send()
    for d in range(4):
        fwd(d).wait_send()
        bwd(d).wait_send()
    for h in range(2):
        cot_copy[h].wait_send()


def hand_over(*refs):
    sources, targets, sem = refs[0:3], refs[3:6], refs[6]
    copies = [pltpu.make_async_copy(sources[i], targets[i], sem.at[i]) for i in range(3)]
    for c in copies:
        c.start()
    for c in copies:
        c.wait()


def per_device_fused(scan_volume, conv_kernel, out_cotangent):
    factor = float(4 * lax.axis_size("sa") * 8 * 128) ** (-0.5)
    f32, bf16 = jnp.float32, jnp.bfloat16
    vmem = pl.BlockSpec(memory_space=pltpu.VMEM)
    act, vgrad, kg = pl.pallas_call(
        functools.partial(fused_kernel, factor),
        out_shape=(pltpu.VMEM((128, 4, 4, 128), bf16), pltpu.VMEM((128, 4, 4, 128), bf16),
                   pltpu.VMEM((3456, 128), f32)),
        in_specs=[pl.BlockSpec(memory_space=pl.ANY)] * 3,
        out_specs=(vmem,) * 3,
        scratch_shapes=[
            pltpu.VMEM((128, 4, 8, 128), bf16), pltpu.VMEM((128, 4, 4, 128), bf16), pltpu.VMEM((27, 128, 128), bf16),
            pltpu.VMEM((128, 4, 4, 128), bf16), pltpu.VMEM((2, 128, 4, 128), bf16),
            pltpu.VMEM((2, 128, 4, 128), bf16), pltpu.VMEM((384, 1152), bf16), pltpu.VMEM((384, 1152), bf16),
            pltpu.VMEM((384, 6144), bf16), pltpu.VMEM((384, 6144), bf16), pltpu.VMEM((384, 4096), bf16),
            pltpu.VMEM((432, 8, 128), f32), pltpu.VMEM((432, 8, 128), bf16),
            pltpu.VMEM((6, 37, 8, 128), bf16), pltpu.VMEM((6, 19, 8, 128), bf16), pltpu.VMEM((6, 10, 8, 128), bf16),
            pltpu.VMEM((6, 37, 8, 128), bf16), pltpu.VMEM((6, 19, 8, 128), bf16), pltpu.VMEM((6, 10, 8, 128), bf16),
            pltpu.VMEM((6, 8, 128), f32),
            pltpu.VMEM((4, 128, 1024), f32), pltpu.VMEM((4, 65, 8, 128), bf16), pltpu.VMEM((4, 65, 8, 128), bf16),
            pltpu.VMEM((4, 128, 1024), f32), pltpu.VMEM((4, 128, 512), f32),
            pltpu.SemaphoreType.DMA((3,)),
            pltpu.SemaphoreType.DMA((6, 6)), pltpu.SemaphoreType.DMA((6, 6)),
            pltpu.SemaphoreType.DMA((4,)), pltpu.SemaphoreType.DMA((4,)),
            pltpu.SemaphoreType.DMA((4,)), pltpu.SemaphoreType.DMA((4,)),
            pltpu.SemaphoreType.DMA((2,)), pltpu.SemaphoreType.DMA((2,)),
            pltpu.SemaphoreType.DMA((8,)), pltpu.SemaphoreType.DMA((8,)),
        ],
        compiler_params=pltpu.CompilerParams(
            collective_id=0, has_side_effects=True, vmem_limit_bytes=56 << 20),
    )(scan_volume, out_cotangent, conv_kernel)
    results = (act, vgrad, kg.reshape(27, 128, 128))
    anywhere = pl.BlockSpec(memory_space=pl.ANY)
    return pl.pallas_call(
        hand_over,
        out_shape=tuple(jax.ShapeDtypeStruct(r.shape, r.dtype) for r in results),
        in_specs=[vmem] * 3,
        out_specs=(anywhere,) * 3,
        scratch_shapes=[pltpu.SemaphoreType.DMA((3,))],
    )(*[pltpu.with_memory_space_constraint(r, pltpu.VMEM) for r in results])


def solution(mesh):
    sizes = (mesh.shape["sa"], mesh.shape["col"], mesh.shape["af"])
    body = per_device_fused if sizes == (8, 2, 2) else per_device
    return jax.shard_map(
        body,
        mesh=mesh,
        in_specs=(P("col", "sa", None, None), P(None, "col", "af"), P("af", "sa", "col", None)),
        out_specs=(P("af", "sa", "col", None), P("col", "sa", "af", None), P(None, "col", "af")),
        check_vma=False,
    )
```
